32 devices in a mesh: seq: 8 (over z, x), head: 4 (over y, core).
Axes of the slice: x: 2, y: 2, z: 4, core: 2. Of those that a mesh axis runs over, the one named last changes fastest.
Arguments:
- teacher_query: bfloat16 [2, 2048, 8192], P(None, ('seq', 'head')), may hold values from -6 to 6
- student_query: bfloat16 [2, 2048, 8192], P(None, ('seq', 'head')), may hold values from -6 to 6
- kept_heads: int32 [40], replicated, may hold values from 0 to 63, as said below
Outputs:
- relation_loss: float32 [2, 64, 2048], P(None, 'head', 'seq')
The draws below stay inside these ranges and needn't reach their ends.
Inputs may be any that keep to these rules, and one draw needn't show every extreme that they name: `kept_heads`: the 40 entries are distinct, and 0 and 63 are among them.
All inputs are finite; a program needn't handle non-finite values.
Results may differ from the reference program's by a relative error of at most 0.0003.
Values may be sent and summed in bfloat16 or wider, within the bound.
No kernel may reach another device: no remote copies, remote signals or barrier semaphores. Data moves between devices by JAX's collectives and lax.ppermute only.
A program may use at most 128 MiB of HBM per device.

```python
import math
import jax
import jax.numpy as jnp
from jax import lax

HEADS = 64
HD = 128
KEPT = 40
RELH = 64
BATCH = 2
SEQ = 2048
TREL = 128
SREL = 80


def query_rows(key, width):
    key_base = jax.random.fold_in(key, 0)
    base = 0.6 * jnp.clip(jax.random.normal(key_base, (SEQ, width), jnp.float32), -5.0, 5.0)
    return base


def batch_rows(key, width):
    seq_keys = jax.random.split(key, BATCH)
    return jnp.stack([query_rows(seq_keys[index], width) for index in range(BATCH)])


def draw_teacher_query(key, part):
    return batch_rows(jax.random.fold_in(key, 1), HEADS * HD).astype(jnp.bfloat16)


def draw_student_query(key, part):
    return batch_rows(jax.random.fold_in(key, 2), HEADS * HD).astype(jnp.bfloat16)


def draw_kept_heads(key, part):
    key_mid, key_order = jax.random.split(jax.random.fold_in(key, 3))
    middle = jax.random.permutation(key_mid, HEADS - 2)[:KEPT - 2] + 1
    chosen = jnp.concatenate([middle.astype(jnp.int32), jnp.array([0, HEADS - 1], jnp.int32)])
    return jax.random.permutation(key_order, chosen).astype(jnp.int32)


def setup_inputs(seed: int = 0) -> dict:
    splits = jax.random.split(jax.random.key(seed), 4)
    return {
        "teacher_query": draw_teacher_query(jax.random.fold_in(splits[3], 71), 0),
        "student_query": draw_student_query(jax.random.fold_in(splits[3], 71), 0),
        "kept_heads": draw_kept_heads(jax.random.fold_in(splits[3], 71), 0),
    }


NEG_FILL = -1.0e30


def one_sequence(teacher_query, student_query, kept_heads):
    picked = jnp.take(student_query.reshape(SEQ, HEADS, HD), kept_heads, axis=1).reshape(SEQ, KEPT * HD)
    teach_all = jnp.transpose(teacher_query.astype(jnp.float32).reshape(SEQ, RELH, TREL), (1, 0, 2))
    stud_all = jnp.transpose(picked.astype(jnp.float32).reshape(SEQ, RELH, SREL), (1, 0, 2))
    block_rows = math.gcd(SEQ, 512)
    positions = jnp.arange(SEQ, dtype=jnp.int32)

    def per_head(pair):
        teach_head, stud_head = pair

        def per_block(block_number):
            row_start = (block_number * block_rows).astype(jnp.int32)
            query_t = lax.dynamic_slice_in_dim(teach_head, row_start, block_rows, 0)
            query_s = lax.dynamic_slice_in_dim(stud_head, row_start, block_rows, 0)
            teach_scores = jnp.dot(query_t, teach_head.T, precision=lax.Precision.HIGHEST, preferred_element_type=jnp.float32) * (TREL ** -0.5)
            stud_scores = jnp.dot(query_s, stud_head.T, precision=lax.Precision.HIGHEST, preferred_element_type=jnp.float32) * (SREL ** -0.5)
            query_pos = row_start + jnp.arange(block_rows, dtype=jnp.int32)
            allowed = positions[None, :] <= query_pos[:, None]
            teach_scores = jnp.where(allowed, teach_scores, NEG_FILL)
            stud_scores = jnp.where(allowed, stud_scores, NEG_FILL)
            log_t = jax.nn.log_softmax(teach_scores, axis=1)
            log_s = jax.nn.log_softmax(stud_scores, axis=1)
            return jnp.sum(jnp.exp(log_t) * (log_t - log_s), axis=1)

        return lax.map(per_block, jnp.arange(SEQ // block_rows, dtype=jnp.int32)).reshape(SEQ)

    return lax.map(per_head, (teach_all, stud_all))


def reference(teacher_query, student_query, kept_heads):
    def per_sequence(pair):
        return one_sequence(pair[0], pair[1], kept_heads)

    return lax.map(per_sequence, (teacher_query, student_query))
```

```python
import functools
import math

import jax
import jax.numpy as jnp
from jax import lax
from jax.experimental import pallas as pl
from jax.experimental.pallas import tpu as pltpu
from jax.sharding import PartitionSpec as P

HEADS = 64
HD = 128
KEPT = 40
RELH = 64
TREL = 128
SREL = 80
LANES = 128
CHUNK = 32
GROUP = 4
BLOCK = 256
LOG2E = math.log2(math.e)
LN2 = math.log(2.0)


def pack_kernel(kept_ref, teach_ref, *refs):
    heads, out_ref = refs[:-1], refs[-1]
    lane = lax.broadcasted_iota(jnp.int32, (2 * HD // 2, LANES), 1)
    small_lane = lax.broadcasted_iota(jnp.int32, (CHUNK, LANES), 1)
    rows = out_ref.shape[3]
    del rows
    picked = [head[...].reshape(LANES, LANES) for head in heads]
    for i in range(GROUP):
        for w in range(2):
            start = (2 * i + w) * TREL
            out_ref[0, i, 0, w * LANES : (w + 1) * LANES, :] = teach_ref[:, :, start : start + TREL].reshape(
                LANES, LANES
            )
        first, last = picked[i], picked[i + 1]
        main = first if i == 0 else jnp.where(lane >= CHUNK * i, first, last)
        out_ref[0, i, 0, 2 * LANES : 3 * LANES, :] = main
        extra = jnp.zeros((CHUNK, LANES), jnp.float32)
        for g in range(4):
            part = last[g * CHUNK : (g + 1) * CHUNK].astype(jnp.float32)
            if g:
                part = pltpu.roll(part, g * CHUNK, 1)
            extra = jnp.where(small_lane // CHUNK == (i + g) % 4, part, extra)
        out_ref[0, i, 0, 3 * LANES :, :] = extra.astype(jnp.bfloat16)


def pack(teacher, student, kept, seq_size, head_size):
    batch, rows, _ = teacher.shape
    message = 3 * LANES + CHUNK
    groups = RELH // (2 * GROUP)

    def out_map(g, kept_ref):
        first = g * GROUP
        return ((first % seq_size) // GROUP, 0, first // seq_size, 0, 0)

    def head_map(m, g, kept_ref):
        return (0, 0, kept_ref[5 * g + m])

    packed = pl.pallas_call(
        pack_kernel,
        out_shape=jax.ShapeDtypeStruct((seq_size // GROUP, GROUP, head_size, message, LANES), jnp.bfloat16),
        grid_spec=pltpu.PrefetchScalarGridSpec(
            num_scalar_prefetch=1,
            grid=(groups,),
            in_specs=[pl.BlockSpec((batch, rows, 2 * GROUP * TREL), lambda g, kept_ref: (0, 0, g))]
            + [pl.BlockSpec((batch, rows, HD), functools.partial(head_map, m)) for m in range(5)],
            out_specs=pl.BlockSpec((1, GROUP, 1, message, LANES), out_map),
        ),
        name="pack_messages",
    )(kept, teacher, *([student] * 5))
    return packed.reshape(seq_size * head_size, message, LANES)


def nt_dot(a, b):
    return lax.dot_general(a, b, (((1,), (1,)), ((), ())), preferred_element_type=jnp.float32)


def relation_kernel(slot_ref, got_ref, out_ref, teach, stud, shift_t, shift_s, acc_t, acc_c, acc_s):
    peers = got_ref.shape[0]
    half = LANES // 2
    count = peers * half
    units = teach.shape[0]
    scale_t = TREL ** (-0.5) * LOG2E
    scale_s = SREL ** (-0.5) * LOG2E
    lane = lax.broadcasted_iota(jnp.int32, (half, LANES), 1)
    rel = (lane - CHUNK * slot_ref[0]) & (LANES - 1)
    in_first = rel < SREL
    in_tail = rel < CHUNK
    zero = jnp.zeros((half, LANES), jnp.float32)

    def unpack(j, carry):
        at = pl.ds(pl.multiple_of(j * half, half), half)
        tail = got_ref[j, 3 * LANES :, :].astype(jnp.float32)
        for b in range(2):
            for w in range(2):
                teach[2 * b + w, at, :] = got_ref[j, w * LANES + b * half : w * LANES + (b + 1) * half, :]
            main = got_ref[j, 2 * LANES + b * half : 2 * LANES + (b + 1) * half, :].astype(jnp.float32)
            parts = [
                pltpu.roll(tail, (LANES - g * CHUNK) % LANES, 1) if g else tail for g in (2 * b, 2 * b + 1)
            ]
            own = jnp.concatenate(parts, axis=0)
            stud[2 * b, at, :] = jnp.where(in_first, main, zero).astype(jnp.bfloat16)
            stud[2 * b + 1, at, :] = jnp.where(in_tail, own, jnp.where(in_first, zero, main)).astype(jnp.bfloat16)
        return carry

    lax.fori_loop(0, peers, unpack, 0)

    ones = jnp.ones((8, LANES), jnp.bfloat16)

    def shifts(ref, u, scale):
        rows = ref[u]
        square = nt_dot(ones, rows * rows)
        norm = jnp.sqrt(square)
        top = jnp.max(norm, axis=1, keepdims=True)
        return norm * (norm + top) * (0.5 * scale)

    key_in = lax.broadcasted_iota(jnp.int32, (BLOCK // 8, 8, BLOCK), 0) * 8 + lax.broadcasted_iota(
        jnp.int32, (BLOCK // 8, 8, BLOCK), 1
    )
    query_in = lax.broadcasted_iota(jnp.int32, (BLOCK // 8, 8, BLOCK), 2)
    allowed = key_in <= query_in

    def unit(u, carry):
        shift_t[...] = shifts(teach, u, scale_t)
        shift_s[...] = shifts(stud, u, scale_s)
        for q in range(count // BLOCK):
            cols = slice(q * BLOCK, (q + 1) * BLOCK)
            query_t = teach[u, cols, :]
            query_s = stud[u, cols, :]
            off_t = shift_t[:, cols]
            off_s = shift_s[:, cols]
            sum_t = jnp.zeros((8, BLOCK), jnp.float32)
            sum_c = jnp.zeros((8, BLOCK), jnp.float32)
            sum_s = jnp.zeros((8, BLOCK), jnp.float32)
            for k in range(q + 1):
                keys = slice(k * BLOCK, (k + 1) * BLOCK)
                x_t = nt_dot(teach[u, keys, :], query_t).reshape(BLOCK // 8, 8, BLOCK) * scale_t - off_t[None]
                x_s = nt_dot(stud[u, keys, :], query_s).reshape(BLOCK // 8, 8, BLOCK) * scale_s - off_s[None]
                w_t = jnp.exp2(x_t)
                w_s = jnp.exp2(x_s)
                if k == q:
                    w_t = jnp.where(allowed, w_t, 0.0)
                    w_s = jnp.where(allowed, w_s, 0.0)
                sum_t += jnp.sum(w_t, axis=0)
                sum_c += jnp.sum(w_t * (x_t - x_s), axis=0)
                sum_s += jnp.sum(w_s, axis=0)
            acc_t[u, q] = sum_t
            acc_c[u, q] = sum_c
            acc_s[u, q] = sum_s
        return carry

    lax.fori_loop(0, units, unit, 0)
    for u in range(units):
        total_t = jnp.sum(acc_t[u], axis=1)
        total_c = jnp.sum(acc_c[u], axis=1)
        total_s = jnp.sum(acc_s[u], axis=1)
        out_ref[:, u, :] = (total_c / total_t - jnp.log2(total_t) + jnp.log2(total_s)) * LN2


def relation(got, slot):
    peers, message, _ = got.shape
    count = peers * LANES // 2
    blocks = count // BLOCK
    units = 4
    return pl.pallas_call(
        relation_kernel,
        out_shape=jax.ShapeDtypeStruct((blocks, units, BLOCK), jnp.float32),
        grid_spec=pltpu.PrefetchScalarGridSpec(
            num_scalar_prefetch=1,
            grid=(1,),
            in_specs=[pl.BlockSpec((peers, message, LANES), lambda i, slot_ref: (0, 0, 0), pipeline_mode=pl.Buffered(1))],
            out_specs=pl.BlockSpec((blocks, units, BLOCK), lambda i, slot_ref: (0, 0, 0)),
            scratch_shapes=[
                pltpu.VMEM((units, count, LANES), jnp.bfloat16),
                pltpu.VMEM((units, count, LANES), jnp.bfloat16),
                pltpu.VMEM((8, count), jnp.float32),
                pltpu.VMEM((8, count), jnp.float32),
                pltpu.VMEM((units, blocks, 8, BLOCK), jnp.float32),
                pltpu.VMEM((units, blocks, 8, BLOCK), jnp.float32),
                pltpu.VMEM((units, blocks, 8, BLOCK), jnp.float32),
            ],
        ),
        compiler_params=pltpu.CompilerParams(vmem_limit_bytes=48 * 1024 * 1024),
        name="relation_loss",
    )(slot, got)


def packed_shards(teacher, student, kept):
    seq_size, head_size = lax.axis_size("seq"), lax.axis_size("head")
    batch = teacher.shape[0]
    messages = pack(teacher, student, kept, seq_size, head_size)
    got = lax.all_to_all(messages, ("seq", "head"), 0, 0, tiled=True)
    slot = (lax.axis_index("seq") % GROUP).astype(jnp.int32).reshape(1)
    mine = relation(got, slot)
    done = lax.all_to_all(mine, "seq", 0, 0, tiled=True)
    pair = RELH // head_size // seq_size
    done = done.reshape(seq_size, batch, pair, BLOCK)
    return jnp.transpose(done, (1, 0, 2, 3)).reshape(batch, RELH // head_size, BLOCK)


NEG_FILL = -1e30


def fresh_stats(head_count, query_count):
    lowest = jnp.full((head_count, query_count), NEG_FILL, jnp.float32)
    zeros_block = jnp.zeros((head_count, query_count), jnp.float32)
    return (lowest, zeros_block, zeros_block, lowest, zeros_block)


def relation_update(running, query_pair, key_pair, query_pos, key_pos, scales):
    top_t, total_t, cross_sum, top_s, total_s = running
    teach_scores = (
        jnp.einsum("qhd,khd->hqk", query_pair[0], key_pair[0], preferred_element_type=jnp.float32)
        * scales[0]
    )
    stud_scores = (
        jnp.einsum("qhd,khd->hqk", query_pair[1], key_pair[1], preferred_element_type=jnp.float32)
        * scales[1]
    )
    allowed = key_pos[None, :] <= query_pos[:, None]
    teach_scores = jnp.where(allowed[None], teach_scores, NEG_FILL)
    stud_scores = jnp.where(allowed[None], stud_scores, NEG_FILL)
    new_top_t = jnp.maximum(top_t, jnp.max(teach_scores, axis=2))
    new_top_s = jnp.maximum(top_s, jnp.max(stud_scores, axis=2))
    weights_t = jnp.exp(teach_scores - new_top_t[:, :, None])
    weights_s = jnp.exp(stud_scores - new_top_s[:, :, None])
    decay_t = jnp.exp(top_t - new_top_t)
    decay_s = jnp.exp(top_s - new_top_s)
    total_t = total_t * decay_t + jnp.sum(weights_t, axis=2)
    cross_sum = cross_sum * decay_t + jnp.sum(weights_t * (teach_scores - stud_scores), axis=2)
    total_s = total_s * decay_s + jnp.sum(weights_s, axis=2)
    return (new_top_t, total_t, cross_sum, new_top_s, total_s)


def finish_rows(running):
    top_t, total_t, cross_sum, top_s, total_s = running
    return cross_sum / total_t - top_t - jnp.log(total_t) + top_s + jnp.log(total_s)


def fold_keys(running, query_pair, query_pos, key_pair, last_query, scales):
    key_length = key_pair[0].shape[0]
    key_block = 512
    steps_total = key_length // key_block

    def one_block(block_number, current):
        row_start = block_number * key_block
        block_t = lax.dynamic_slice_in_dim(key_pair[0], row_start, key_block, 0)
        block_s = lax.dynamic_slice_in_dim(key_pair[1], row_start, key_block, 0)
        key_pos = row_start + jnp.arange(key_block, dtype=jnp.int32)
        return relation_update(current, query_pair, (block_t, block_s), query_pos, key_pos, scales)

    needed = jnp.clip(last_query // key_block + 1, 0, steps_total)
    return lax.fori_loop(0, needed, one_block, running)


def batch_inside(local, head_count, width):
    seq_count_b, rows, columns = local.shape
    folded = local.reshape(seq_count_b, rows, head_count, width)
    return jnp.transpose(folded, (1, 0, 2, 3)).reshape(rows, seq_count_b * head_count * width)


def shards(teacher_query, student_query, kept_heads):
    batch_count = student_query.shape[0]
    token_rows = student_query.shape[1]
    split_heads = student_query.reshape(batch_count, token_rows, HEADS, HD)
    picked = jnp.take(split_heads, kept_heads, axis=2).reshape(batch_count, token_rows, KEPT * HD)
    teach_local, stud_local = (
        lax.all_to_all(teacher_query, "head", split_axis=2, concat_axis=1, tiled=True),
        lax.all_to_all(picked, "head", split_axis=2, concat_axis=1, tiled=True),
    )
    local_rows = teach_local.shape[1]
    head_count = RELH // lax.axis_size("head")
    wide_heads = batch_count * head_count
    teach_flat = batch_inside(teach_local, head_count, TREL)
    stud_flat = batch_inside(stud_local, head_count, SREL)
    position = lax.axis_index("seq")
    scales = (TREL ** (-0.5), SREL ** (-0.5))
    teach_heads = teach_flat.reshape(local_rows, wide_heads, TREL)
    stud_heads = stud_flat.reshape(local_rows, wide_heads, SREL)
    query_pos = position * local_rows + jnp.arange(local_rows, dtype=jnp.int32)
    last_query = position * local_rows + local_rows - 1
    key_pair = (
        lax.all_gather(teach_flat, "seq", axis=0, tiled=True).reshape(-1, wide_heads, TREL),
        lax.all_gather(stud_flat, "seq", axis=0, tiled=True).reshape(-1, wide_heads, SREL),
    )
    running = fold_keys(
        fresh_stats(wide_heads, local_rows),
        (teach_heads, stud_heads),
        query_pos,
        key_pair,
        last_query,
        scales,
    )
    return finish_rows(running).reshape(batch_count, head_count, local_rows)


def solution(mesh):
    placed = (P(None, ("seq", "head"), None), P(None, ("seq", "head"), None), P())
    sizes = dict(mesh.shape)

    def run(teacher, student, kept):
        seq_size, head_size = sizes["seq"], sizes["head"]
        batch, length = teacher.shape[0], teacher.shape[1]
        rows = length // (seq_size * head_size)
        fits = (
            batch * rows == LANES
            and batch == 2
            and seq_size % GROUP == 0
            and RELH == 2 * seq_size * head_size
            and length // seq_size == BLOCK
        )
        return jax.shard_map(
            packed_shards if fits else shards,
            mesh=mesh,
            in_specs=placed,
            out_specs=P(None, "head", "seq"),
            check_vma=False,
        )(teacher, student, kept)

    return run
```

```python
import functools
import math

import jax
import jax.numpy as jnp
from jax import lax
from jax.experimental import pallas as pl
from jax.experimental.pallas import tpu as pltpu
from jax.sharding import PartitionSpec as P

HEADS = 64
HD = 128
KEPT = 40
RELH = 64
TREL = 128
SREL = 80
LANES = 128
CHUNK = 32
GROUP = 4
BLOCK = 256
LIMIT = 6.0
LOG2E = math.log2(math.e)
LN2 = math.log(2.0)
SCALE_T = TREL ** (-0.5) * LOG2E
SCALE_S = SREL ** (-0.5) * LOG2E


def pack_kernel(kept_ref, teach_ref, *refs):
    heads, out_ref = refs[:-1], refs[-1]
    lane = lax.broadcasted_iota(jnp.int32, (2 * HD // 2, LANES), 1)
    small_lane = lax.broadcasted_iota(jnp.int32, (CHUNK, LANES), 1)
    picked = [head[...].reshape(LANES, LANES) for head in heads]
    for i in range(GROUP):
        for w in range(2):
            start = (2 * i + w) * TREL
            out_ref[0, i, 0, w * LANES : (w + 1) * LANES, :] = teach_ref[:, :, start : start + TREL].reshape(
                LANES, LANES
            )
        first, last = picked[i], picked[i + 1]
        main = first if i == 0 else jnp.where(lane >= CHUNK * i, first, last)
        out_ref[0, i, 0, 2 * LANES : 3 * LANES, :] = main
        extra = jnp.zeros((CHUNK, LANES), jnp.float32)
        for g in range(4):
            part = last[g * CHUNK : (g + 1) * CHUNK].astype(jnp.float32)
            if g:
                part = pltpu.roll(part, g * CHUNK, 1)
            extra = jnp.where(small_lane // CHUNK == (i + g) % 4, part, extra)
        out_ref[0, i, 0, 3 * LANES :, :] = extra.astype(jnp.bfloat16)


def pack(teacher, student, kept, seq_size, head_size):
    batch, rows, _ = teacher.shape
    message = 3 * LANES + CHUNK
    groups = RELH // (2 * GROUP)

    def out_map(g, kept_ref):
        first = g * GROUP
        return ((first % seq_size) // GROUP, 0, first // seq_size, 0, 0)

    def head_map(m, g, kept_ref):
        return (0, 0, kept_ref[5 * g + m])

    packed = pl.pallas_call(
        pack_kernel,
        out_shape=jax.ShapeDtypeStruct((seq_size // GROUP, GROUP, head_size, message, LANES), jnp.bfloat16),
        grid_spec=pltpu.PrefetchScalarGridSpec(
            num_scalar_prefetch=1,
            grid=(groups,),
            in_specs=[pl.BlockSpec((batch, rows, 2 * GROUP * TREL), lambda g, kept_ref: (0, 0, g))]
            + [pl.BlockSpec((batch, rows, HD), functools.partial(head_map, m)) for m in range(5)],
            out_specs=pl.BlockSpec((1, GROUP, 1, message, LANES), out_map),
        ),
        name="pack_messages",
    )(kept, teacher, *([student] * 5))
    return packed.reshape(seq_size * head_size, message, LANES)


def nt_dot(a, b):
    return lax.dot_general(a, b, (((1,), (1,)), ((), ())), preferred_element_type=jnp.float32)


def shift_of(rows, width, factor):
    norm = jnp.sqrt(nt_dot(jnp.ones((8, LANES), jnp.bfloat16), rows * rows))
    return norm * (norm + LIMIT * math.sqrt(width)) * (0.5 * factor)


def tile_sums(key_t, key_s, query_t, query_s, off_t, off_s, allowed):
    tile = (BLOCK // 8, 8, BLOCK)
    x_t = nt_dot(jnp.concatenate([key_t, key_t], axis=1), query_t).reshape(tile) - off_t[None]
    x_s = nt_dot(jnp.concatenate([key_s, key_s], axis=1), query_s).reshape(tile) - off_s[None]
    w_t = jnp.exp2(x_t)
    w_s = jnp.exp2(x_s)
    if allowed is not None:
        w_t = jnp.where(allowed, w_t, 0.0)
        w_s = jnp.where(allowed, w_s, 0.0)
    return jnp.sum(w_t, axis=0), jnp.sum(w_t * (x_t - x_s), axis=0), jnp.sum(w_s, axis=0)


def causal_tile():
    tile = (BLOCK // 8, 8, BLOCK)
    key_in = lax.broadcasted_iota(jnp.int32, tile, 0) * 8 + lax.broadcasted_iota(jnp.int32, tile, 1)
    return key_in <= lax.broadcasted_iota(jnp.int32, tile, 2)


def split_terms(row, scale):
    scaled = row * scale
    high = scaled.astype(jnp.bfloat16)
    return high, (scaled - high.astype(jnp.float32)).astype(jnp.bfloat16)


def relation_kernel(slot_ref, got_ref, out_ref, teach, stud, query_t, query_s, shifts, acc_t, acc_c, acc_s):
    peers = got_ref.shape[0]
    half = LANES // 2
    count = peers * half
    units = teach.shape[0]
    lane = lax.broadcasted_iota(jnp.int32, (half, LANES), 1)
    rel = (lane - CHUNK * slot_ref[0]) & (LANES - 1)
    in_first = rel < SREL
    in_tail = rel < CHUNK
    zero = jnp.zeros((half, LANES), jnp.float32)

    def unpack(j, carry):
        at = pl.ds(pl.multiple_of(j * half, half), half)
        tail = got_ref[j, 3 * LANES :, :].astype(jnp.float32)
        for b in range(2):
            for w in range(2):
                key = got_ref[j, w * LANES + b * half : w * LANES + (b + 1) * half, :]
                u = 2 * b + w
                teach[u, at, :] = key
                query_t[u, at, 0:LANES], query_t[u, at, LANES:] = split_terms(key.astype(jnp.float32), SCALE_T)
            main = got_ref[j, 2 * LANES + b * half : 2 * LANES + (b + 1) * half, :].astype(jnp.float32)
            parts = [
                pltpu.roll(tail, (LANES - g * CHUNK) % LANES, 1) if g else tail for g in (2 * b, 2 * b + 1)
            ]
            own = jnp.concatenate(parts, axis=0)
            both = (jnp.where(in_first, main, zero), jnp.where(in_tail, own, jnp.where(in_first, zero, main)))
            for w, row in enumerate(both):
                u = 2 * b + w
                stud[u, at, :] = row.astype(jnp.bfloat16)
                query_s[u, at, 0:LANES], query_s[u, at, LANES:] = split_terms(row, SCALE_S)
        return carry

    lax.fori_loop(0, peers, unpack, 0)
    allowed = causal_tile()

    def shift(u, carry):
        shifts[u, 0] = shift_of(teach[u], TREL, SCALE_T)
        shifts[u, 1] = shift_of(stud[u], SREL, SCALE_S)
        return carry

    lax.fori_loop(0, units, shift, 0)

    def unit(u, carry):
        for q in range(count // BLOCK):
            cols = slice(q * BLOCK, (q + 1) * BLOCK)
            sums = [jnp.zeros((8, BLOCK), jnp.float32)] * 3
            for k in range(q + 1):
                keys = slice(k * BLOCK, (k + 1) * BLOCK)
                more = tile_sums(
                    teach[u, keys, :],
                    stud[u, keys, :],
                    query_t[u, cols, :],
                    query_s[u, cols, :],
                    shifts[u, 0, :, cols],
                    shifts[u, 1, :, cols],
                    allowed if k == q else None,
                )
                sums = [a + b for a, b in zip(sums, more)]
            acc_t[u, q], acc_c[u, q], acc_s[u, q] = sums
        return carry

    lax.fori_loop(0, units, unit, 0)
    for u in range(units):
        total_t = jnp.sum(acc_t[u], axis=1)
        total_c = jnp.sum(acc_c[u], axis=1)
        total_s = jnp.sum(acc_s[u], axis=1)
        out_ref[:, u, :] = (total_c / total_t - jnp.log2(total_t) + jnp.log2(total_s)) * LN2


def relation(got, slot):
    peers, message, _ = got.shape
    count = peers * LANES // 2
    blocks = count // BLOCK
    units = 4
    return pl.pallas_call(
        relation_kernel,
        out_shape=jax.ShapeDtypeStruct((blocks, units, BLOCK), jnp.float32),
        grid_spec=pltpu.PrefetchScalarGridSpec(
            num_scalar_prefetch=1,
            grid=(1,),
            in_specs=[pl.BlockSpec((peers, message, LANES), lambda i, slot_ref: (0, 0, 0), pipeline_mode=pl.Buffered(1))],
            out_specs=pl.BlockSpec((blocks, units, BLOCK), lambda i, slot_ref: (0, 0, 0)),
            scratch_shapes=[
                pltpu.VMEM((units, count, LANES), jnp.bfloat16),
                pltpu.VMEM((units, count, LANES), jnp.bfloat16),
                pltpu.VMEM((units, count, 2 * LANES), jnp.bfloat16),
                pltpu.VMEM((units, count, 2 * LANES), jnp.bfloat16),
                pltpu.VMEM((units, 2, 8, count), jnp.float32),
                pltpu.VMEM((units, blocks, 8, BLOCK), jnp.float32),
                pltpu.VMEM((units, blocks, 8, BLOCK), jnp.float32),
                pltpu.VMEM((units, blocks, 8, BLOCK), jnp.float32),
            ],
        ),
        compiler_params=pltpu.CompilerParams(vmem_limit_bytes=48 * 1024 * 1024),
        name="relation_loss",
    )(slot, got)


def packed_shards(teacher, student, kept):
    seq_size, head_size = lax.axis_size("seq"), lax.axis_size("head")
    batch = teacher.shape[0]
    messages = pack(teacher, student, kept, seq_size, head_size)
    got = lax.all_to_all(messages, ("seq", "head"), 0, 0, tiled=True)
    slot = (lax.axis_index("seq") % GROUP).astype(jnp.int32).reshape(1)
    mine = relation(got, slot)
    done = lax.all_to_all(mine, "seq", 0, 0, tiled=True)
    pair = RELH // head_size // seq_size
    done = done.reshape(seq_size, batch, pair, BLOCK)
    return jnp.transpose(done, (1, 0, 2, 3)).reshape(batch, RELH // head_size, BLOCK)


NEG_FILL = -1e30


def fresh_stats(head_count, query_count):
    lowest = jnp.full((head_count, query_count), NEG_FILL, jnp.float32)
    zeros_block = jnp.zeros((head_count, query_count), jnp.float32)
    return (lowest, zeros_block, zeros_block, lowest, zeros_block)


def relation_update(running, query_pair, key_pair, query_pos, key_pos, scales):
    top_t, total_t, cross_sum, top_s, total_s = running
    teach_scores = (
        jnp.einsum("qhd,khd->hqk", query_pair[0], key_pair[0], preferred_element_type=jnp.float32)
        * scales[0]
    )
    stud_scores = (
        jnp.einsum("qhd,khd->hqk", query_pair[1], key_pair[1], preferred_element_type=jnp.float32)
        * scales[1]
    )
    allowed = key_pos[None, :] <= query_pos[:, None]
    teach_scores = jnp.where(allowed[None], teach_scores, NEG_FILL)
    stud_scores = jnp.where(allowed[None], stud_scores, NEG_FILL)
    new_top_t = jnp.maximum(top_t, jnp.max(teach_scores, axis=2))
    new_top_s = jnp.maximum(top_s, jnp.max(stud_scores, axis=2))
    weights_t = jnp.exp(teach_scores - new_top_t[:, :, None])
    weights_s = jnp.exp(stud_scores - new_top_s[:, :, None])
    decay_t = jnp.exp(top_t - new_top_t)
    decay_s = jnp.exp(top_s - new_top_s)
    total_t = total_t * decay_t + jnp.sum(weights_t, axis=2)
    cross_sum = cross_sum * decay_t + jnp.sum(weights_t * (teach_scores - stud_scores), axis=2)
    total_s = total_s * decay_s + jnp.sum(weights_s, axis=2)
    return (new_top_t, total_t, cross_sum, new_top_s, total_s)


def finish_rows(running):
    top_t, total_t, cross_sum, top_s, total_s = running
    return cross_sum / total_t - top_t - jnp.log(total_t) + top_s + jnp.log(total_s)


def fold_keys(running, query_pair, query_pos, key_pair, last_query, scales):
    key_length = key_pair[0].shape[0]
    key_block = 512
    steps_total = key_length // key_block

    def one_block(block_number, current):
        row_start = block_number * key_block
        block_t = lax.dynamic_slice_in_dim(key_pair[0], row_start, key_block, 0)
        block_s = lax.dynamic_slice_in_dim(key_pair[1], row_start, key_block, 0)
        key_pos = row_start + jnp.arange(key_block, dtype=jnp.int32)
        return relation_update(current, query_pair, (block_t, block_s), query_pos, key_pos, scales)

    needed = jnp.clip(last_query // key_block + 1, 0, steps_total)
    return lax.fori_loop(0, needed, one_block, running)


def batch_inside(local, head_count, width):
    seq_count_b, rows, columns = local.shape
    folded = local.reshape(seq_count_b, rows, head_count, width)
    return jnp.transpose(folded, (1, 0, 2, 3)).reshape(rows, seq_count_b * head_count * width)


def shards(teacher_query, student_query, kept_heads):
    batch_count = student_query.shape[0]
    token_rows = student_query.shape[1]
    split_heads = student_query.reshape(batch_count, token_rows, HEADS, HD)
    picked = jnp.take(split_heads, kept_heads, axis=2).reshape(batch_count, token_rows, KEPT * HD)
    teach_local, stud_local = (
        lax.all_to_all(teacher_query, "head", split_axis=2, concat_axis=1, tiled=True),
        lax.all_to_all(picked, "head", split_axis=2, concat_axis=1, tiled=True),
    )
    local_rows = teach_local.shape[1]
    head_count = RELH // lax.axis_size("head")
    wide_heads = batch_count * head_count
    teach_flat = batch_inside(teach_local, head_count, TREL)
    stud_flat = batch_inside(stud_local, head_count, SREL)
    position = lax.axis_index("seq")
    scales = (TREL ** (-0.5), SREL ** (-0.5))
    teach_heads = teach_flat.reshape(local_rows, wide_heads, TREL)
    stud_heads = stud_flat.reshape(local_rows, wide_heads, SREL)
    query_pos = position * local_rows + jnp.arange(local_rows, dtype=jnp.int32)
    last_query = position * local_rows + local_rows - 1
    key_pair = (
        lax.all_gather(teach_flat, "seq", axis=0, tiled=True).reshape(-1, wide_heads, TREL),
        lax.all_gather(stud_flat, "seq", axis=0, tiled=True).reshape(-1, wide_heads, SREL),
    )
    running = fold_keys(
        fresh_stats(wide_heads, local_rows),
        (teach_heads, stud_heads),
        query_pos,
        key_pair,
        last_query,
        scales,
    )
    return finish_rows(running).reshape(batch_count, head_count, local_rows)


def solution(mesh):
    placed = (P(None, ("seq", "head"), None), P(None, ("seq", "head"), None), P())
    sizes = dict(mesh.shape)

    def run(teacher, student, kept):
        seq_size, head_size = sizes["seq"], sizes["head"]
        batch, length = teacher.shape[0], teacher.shape[1]
        rows = length // (seq_size * head_size)
        fits = (
            batch * rows == LANES
            and batch == 2
            and seq_size % GROUP == 0
            and RELH == 2 * seq_size * head_size
            and length // seq_size == BLOCK
        )
        return jax.shard_map(
            packed_shards if fits else shards,
            mesh=mesh,
            in_specs=placed,
            out_specs=P(None, "head", "seq"),
            check_vma=False,
        )(teacher, student, kept)

    return run
```

```python
import functools
import math

import jax
import jax.numpy as jnp
from jax import lax
from jax.experimental import pallas as pl
from jax.experimental.pallas import tpu as pltpu
from jax.sharding import PartitionSpec as P


HEADS = 64
HD = 128
KEPT = 40
RELH = 64
TREL = 128
SREL = 80
LANES = 128
CHUNK = 32
GROUP = 4
BLOCK = 256
LIMIT = 6.0
LOG2E = math.log2(math.e)
LN2 = math.log(2.0)
SCALE_T = TREL ** (-0.5) * LOG2E
SCALE_S = SREL ** (-0.5) * LOG2E


SEQ_SIZE = 8
STAGES = ((0, 2), (4, 2), (2, 2), (6, 1), (7, 1))
HEAD_SIZE = 4
MESSAGE = 3 * LANES + CHUNK
UNITS = 4
ROWS = 64


def pack_kernel(cross, kept_ref, teach_hbm, stud_hbm, *refs):
    outs = refs[-19:-3]
    teach, heads, sems = refs[-3:]
    seq, head = lax.axis_index("seq"), lax.axis_index("head")
    lane = lax.broadcasted_iota(jnp.int32, (LANES, LANES), 1)
    small_lane = lax.broadcasted_iota(jnp.int32, (CHUNK, LANES), 1)
    copies = []
    for turn in range(HEAD_SIZE):
        group = 2 * (head ^ turn) + ((seq >> 2) ^ cross)
        width = 2 * GROUP * TREL
        some = [
            pltpu.make_async_copy(
                teach_hbm.at[:, :, pl.ds(pl.multiple_of(group * width, width), width)],
                teach.at[turn],
                sems.at[turn, 0],
            )
        ]
        for m in range(5):
            start = pl.multiple_of(kept_ref[5 * group + m] * HD, HD)
            some.append(
                pltpu.make_async_copy(
                    stud_hbm.at[:, :, pl.ds(start, HD)], heads.at[turn, m], sems.at[turn, m + 1]
                )
            )
        for copy in some:
            copy.start()
        copies.append(some)
    for turn in range(HEAD_SIZE):
        for copy in copies[turn]:
            copy.wait()
        for step in range(GROUP):
            i = (seq & 3) ^ step
            out = outs[GROUP * step + turn]
            for w in range(2):
                start = pl.multiple_of((2 * i + w) * TREL, TREL)
                out[w * LANES : (w + 1) * LANES, :] = teach[turn, :, :, pl.ds(start, TREL)].reshape(LANES, LANES)
            first = heads[turn, i].reshape(LANES, LANES)
            last = heads[turn, i + 1].reshape(LANES, LANES)
            out[2 * LANES : 3 * LANES, :] = jnp.where(lane >= CHUNK * i, first, last)
            extra = jnp.zeros((CHUNK, LANES), jnp.float32)
            for g in range(4):
                part = last[g * CHUNK : (g + 1) * CHUNK].astype(jnp.float32)
                if g:
                    part = pltpu.roll(part, g * CHUNK, 1)
                extra = jnp.where(small_lane // CHUNK == ((i + g) & 3), part, extra)
            out[3 * LANES :, :] = extra.astype(jnp.bfloat16)


def pack(cross, kept, teacher, student, after=()):
    anywhere = pl.BlockSpec(memory_space=pl.ANY)
    return pl.pallas_call(
        functools.partial(pack_kernel, cross),
        out_shape=[jax.ShapeDtypeStruct((MESSAGE, LANES), jnp.bfloat16)] * 16,
        grid_spec=pltpu.PrefetchScalarGridSpec(
            num_scalar_prefetch=1,
            grid=(1,),
            in_specs=[anywhere] * (2 + len(after)),
            out_specs=[whole_block((MESSAGE, LANES))] * 16,
            scratch_shapes=[
                pltpu.VMEM((HEAD_SIZE, 2, ROWS, 2 * GROUP * TREL), jnp.bfloat16),
                pltpu.VMEM((HEAD_SIZE, 5, 2, ROWS, HD), jnp.bfloat16),
                pltpu.SemaphoreType.DMA((HEAD_SIZE, 6)),
            ],
        ),
        name="pack_cross" if cross else "pack_near",
    )(kept, teacher, student, *after)


def whole_block(shape):
    return pl.BlockSpec(shape, lambda *_: (0,) * len(shape), pipeline_mode=pl.Buffered(1))


def nt_dot(a, b):
    return lax.dot_general(a, b, (((1,), (1,)), ((), ())), preferred_element_type=jnp.float32)


def shift_of(rows, width, factor):
    norm = jnp.sqrt(nt_dot(jnp.ones((8, LANES), jnp.bfloat16), rows * rows))
    return norm * (norm + LIMIT * math.sqrt(width)) * (0.5 * factor)


def split_terms(row, scale):
    scaled = row * scale
    high = scaled.astype(jnp.bfloat16)
    return high, (scaled - high.astype(jnp.float32)).astype(jnp.bfloat16)


def prepared_shapes(blocks):
    count = blocks * BLOCK
    bf16 = jnp.bfloat16
    return [
        ((UNITS, count, LANES), bf16),
        ((UNITS, count, LANES), bf16),
        ((UNITS, count, 2 * LANES), bf16),
        ((UNITS, count, 2 * LANES), bf16),
        ((UNITS, 2, blocks, 8, BLOCK), jnp.float32),
    ]


def prepare(messages, made):
    key_t, key_s, query_t, query_s, shifts = made
    lane = lax.broadcasted_iota(jnp.int32, (ROWS, LANES), 1)
    rel = (lane - CHUNK * (lax.axis_index("seq") & 3)) & (LANES - 1)
    in_first = rel < SREL
    in_tail = rel < CHUNK
    zero = jnp.zeros((ROWS, LANES), jnp.float32)
    for k, message in enumerate(messages):
        start = (k // 4) * BLOCK + (lax.axis_index("head") ^ (k % 4)) * ROWS
        at = pl.ds(pl.multiple_of(start, ROWS), ROWS)
        tail = message[3 * LANES :, :].astype(jnp.float32)
        for b in range(2):
            main = message[2 * LANES + b * ROWS : 2 * LANES + (b + 1) * ROWS, :].astype(jnp.float32)
            parts = [
                pltpu.roll(tail, LANES - g * CHUNK, 1) if g else tail for g in (2 * b, 2 * b + 1)
            ]
            own = jnp.concatenate(parts, axis=0)
            both = (jnp.where(in_first, main, zero), jnp.where(in_tail, own, jnp.where(in_first, zero, main)))
            for w in range(2):
                u = 2 * b + w
                key = message[w * LANES + b * ROWS : w * LANES + (b + 1) * ROWS, :]
                key_t[u, at, :] = key
                query_t[u, at, 0:LANES], query_t[u, at, LANES:] = split_terms(key.astype(jnp.float32), SCALE_T)
                key_s[u, at, :] = both[w].astype(jnp.bfloat16)
                query_s[u, at, 0:LANES], query_s[u, at, LANES:] = split_terms(both[w], SCALE_S)

    def shift(u, carry):
        for block in range(len(messages) // 4):
            rows = slice(block * BLOCK, (block + 1) * BLOCK)
            shifts[u, 0, block] = shift_of(key_t[u, rows, :], TREL, SCALE_T)
            shifts[u, 1, block] = shift_of(key_s[u, rows, :], SREL, SCALE_S)
        return carry

    lax.fori_loop(0, UNITS, shift, 0)


def tile_sums(u, keys, key_block, queries, query_block, allowed=None):
    rows = pl.ds(pl.multiple_of(key_block * BLOCK, BLOCK), BLOCK)
    cols = pl.ds(pl.multiple_of(query_block * BLOCK, BLOCK), BLOCK)
    tile = (BLOCK // 8, 8, BLOCK)
    key_t, key_s = keys[0][u, rows, :], keys[1][u, rows, :]
    x_t = nt_dot(jnp.concatenate([key_t, key_t], axis=1), queries[2][u, cols, :])
    x_s = nt_dot(jnp.concatenate([key_s, key_s], axis=1), queries[3][u, cols, :])
    x_t = x_t.reshape(tile) - queries[4][u, 0, query_block][None]
    x_s = x_s.reshape(tile) - queries[4][u, 1, query_block][None]
    w_t = jnp.exp2(x_t)
    w_s = jnp.exp2(x_s)
    if allowed is not None:
        w_t = jnp.where(allowed, w_t, 0.0)
        w_s = jnp.where(allowed, w_s, 0.0)
    return jnp.sum(w_t, axis=0), jnp.sum(w_t * (x_t - x_s), axis=0), jnp.sum(w_s, axis=0)


def causal_tile():
    tile = (BLOCK // 8, 8, BLOCK)
    key_in = lax.broadcasted_iota(jnp.int32, tile, 0) * 8 + lax.broadcasted_iota(jnp.int32, tile, 1)
    return key_in <= lax.broadcasted_iota(jnp.int32, tile, 2)


def over_units(tiles, body):
    some = max(1, min(UNITS, 8 // tiles))

    def step(i, carry):
        for j in range(some):
            body(i * some + j)
        return carry

    if some == UNITS:
        step(0, 0)
    else:
        lax.fori_loop(0, UNITS // some, step, 0)


def add_to(sums, slot, u, more):
    for i in range(3):
        sums[slot, u, i] += more[i]


def pairs_inside(seq, base, blocks, made, sums):
    allowed = causal_tile()

    def unit(u):
        for m in range(blocks):
            for n in range(m + 1, blocks):
                ahead = (seq ^ (base + m)) < (seq ^ (base + n))
                key_block = jnp.where(ahead, m, n)
                query_block = jnp.where(ahead, n, m)
                add_to(sums, base + query_block, u, tile_sums(u, made, key_block, made, query_block))
        for m in range(blocks):
            add_to(sums, base + m, u, tile_sums(u, made, m, made, m, allowed))

    over_units(blocks * (blocks + 1) // 2, unit)


def pairs_between(seq, old_base, old_blocks, old, new_base, new_blocks, new, sums):
    ahead = (seq ^ old_base) < (seq ^ new_base)

    def old_keys(u):
        for n in range(new_blocks):
            parts = [tile_sums(u, old, m, new, n) for m in range(old_blocks)]
            add_to(sums, new_base + n, u, [sum(part[i] for part in parts) for i in range(3)])

    def new_keys(u):
        for m in range(old_blocks):
            parts = [tile_sums(u, new, n, old, m) for n in range(new_blocks)]
            add_to(sums, old_base + m, u, [sum(part[i] for part in parts) for i in range(3)])

    @pl.when(ahead)
    def _():
        over_units(old_blocks * new_blocks, old_keys)

    @pl.when(jnp.logical_not(ahead))
    def _():
        over_units(old_blocks * new_blocks, new_keys)


def stage_kernel(base, blocks, older, last, *refs):
    messages, refs = refs[: 4 * blocks], refs[4 * blocks :]
    sets = []
    for start, size in older:
        sets.append((start, size, refs[:5]))
        refs = refs[5:]
    before = None
    if older:
        before, refs = refs[0], refs[1:]
    if last:
        out_ref, made, sums = refs[0], refs[1:6], refs[6]
    else:
        made, sums = refs[:5], refs[5]
    seq = lax.axis_index("seq")
    sums[...] = jnp.zeros(sums.shape, jnp.float32) if before is None else before[...]
    prepare(messages, made)
    for start, size, old in sets:
        pairs_between(seq, start, size, old, base, blocks, made, sums)
    pairs_inside(seq, base, blocks, made, sums)
    if last:
        for m in range(SEQ_SIZE):
            total = jnp.sum(sums[m], axis=2)
            total_t, total_c, total_s = total[:, 0], total[:, 1], total[:, 2]
            out_ref[seq ^ m] = (total_c / total_t - jnp.log2(total_t) + jnp.log2(total_s)) * LN2


def stage(base, blocks, older, messages, old_sets, before, last=False):
    made_shapes = prepared_shapes(blocks)
    sums_shape = (SEQ_SIZE, UNITS, 3, 8, BLOCK)
    out_shape = (SEQ_SIZE, UNITS, BLOCK)
    if last:
        outs, scratch = [(out_shape, jnp.float32)], made_shapes + [(sums_shape, jnp.float32)]
    else:
        outs, scratch = made_shapes + [(sums_shape, jnp.float32)], []
    inputs = list(messages) + [array for old in old_sets for array in old] + ([before] if older else [])
    return pl.pallas_call(
        functools.partial(stage_kernel, base, blocks, older, last),
        out_shape=[jax.ShapeDtypeStruct(shape, dtype) for shape, dtype in outs],
        grid_spec=pl.GridSpec(
            grid=(1,),
            in_specs=[whole_block(array.shape) for array in inputs],
            out_specs=[whole_block(shape) for shape, _ in outs],
            scratch_shapes=[pltpu.VMEM(shape, dtype) for shape, dtype in scratch],
        ),
        compiler_params=pltpu.CompilerParams(vmem_limit_bytes=24 * 1024 * 1024),
    )(*inputs)


def packed_shards(teacher, student, kept):
    batch = teacher.shape[0]

    def exchange(message, k):
        pairs = [(i, i ^ k) for i in range(SEQ_SIZE * HEAD_SIZE)]
        return lax.ppermute(message, ("seq", "head"), pairs)

    far = pack(1, kept, teacher, student)
    got = {}
    for k in range(16, 32):
        got[k] = exchange(far[k - 16], k)
    near = pack(0, kept, teacher, student, (far[15],))
    got[0] = near[0]
    for k in range(1, 16):
        got[k] = exchange(near[k], k)
    messages = [got[k] for k in range(32)]
    older, sums = [], None
    for base, blocks in STAGES:
        *made, sums = stage(
            base,
            blocks,
            tuple(entry[:2] for entry in older),
            messages[4 * base : 4 * (base + blocks)],
            [entry[2] for entry in older],
            sums,
            last=(base, blocks) == STAGES[-1],
        )
        older.append((base, blocks, made))
    mine = sums
    done = lax.all_to_all(mine, "seq", 0, 0, tiled=True)
    pair = RELH // HEAD_SIZE // SEQ_SIZE
    done = done.reshape(SEQ_SIZE, batch, pair, BLOCK)
    return jnp.transpose(done, (1, 0, 2, 3)).reshape(batch, RELH // HEAD_SIZE, BLOCK)


NEG_FILL = -1e30


def fresh_stats(head_count, query_count):
    lowest = jnp.full((head_count, query_count), NEG_FILL, jnp.float32)
    zeros_block = jnp.zeros((head_count, query_count), jnp.float32)
    return (lowest, zeros_block, zeros_block, lowest, zeros_block)


def relation_update(running, query_pair, key_pair, query_pos, key_pos, scales):
    top_t, total_t, cross_sum, top_s, total_s = running
    teach_scores = (
        jnp.einsum("qhd,khd->hqk", query_pair[0], key_pair[0], preferred_element_type=jnp.float32)
        * scales[0]
    )
    stud_scores = (
        jnp.einsum("qhd,khd->hqk", query_pair[1], key_pair[1], preferred_element_type=jnp.float32)
        * scales[1]
    )
    allowed = key_pos[None, :] <= query_pos[:, None]
    teach_scores = jnp.where(allowed[None], teach_scores, NEG_FILL)
    stud_scores = jnp.where(allowed[None], stud_scores, NEG_FILL)
    new_top_t = jnp.maximum(top_t, jnp.max(teach_scores, axis=2))
    new_top_s = jnp.maximum(top_s, jnp.max(stud_scores, axis=2))
    weights_t = jnp.exp(teach_scores - new_top_t[:, :, None])
    weights_s = jnp.exp(stud_scores - new_top_s[:, :, None])
    decay_t = jnp.exp(top_t - new_top_t)
    decay_s = jnp.exp(top_s - new_top_s)
    total_t = total_t * decay_t + jnp.sum(weights_t, axis=2)
    cross_sum = cross_sum * decay_t + jnp.sum(weights_t * (teach_scores - stud_scores), axis=2)
    total_s = total_s * decay_s + jnp.sum(weights_s, axis=2)
    return (new_top_t, total_t, cross_sum, new_top_s, total_s)


def finish_rows(running):
    top_t, total_t, cross_sum, top_s, total_s = running
    return cross_sum / total_t - top_t - jnp.log(total_t) + top_s + jnp.log(total_s)


def fold_keys(running, query_pair, query_pos, key_pair, last_query, scales):
    key_length = key_pair[0].shape[0]
    key_block = 512
    steps_total = key_length // key_block

    def one_block(block_number, current):
        row_start = block_number * key_block
        block_t = lax.dynamic_slice_in_dim(key_pair[0], row_start, key_block, 0)
        block_s = lax.dynamic_slice_in_dim(key_pair[1], row_start, key_block, 0)
        key_pos = row_start + jnp.arange(key_block, dtype=jnp.int32)
        return relation_update(current, query_pair, (block_t, block_s), query_pos, key_pos, scales)

    needed = jnp.clip(last_query // key_block + 1, 0, steps_total)
    return lax.fori_loop(0, needed, one_block, running)


def batch_inside(local, head_count, width):
    seq_count_b, rows, _ = local.shape
    folded = local.reshape(seq_count_b, rows, head_count, width)
    return jnp.transpose(folded, (1, 0, 2, 3)).reshape(rows, seq_count_b * head_count * width)


def shards(teacher_query, student_query, kept_heads):
    batch_count = student_query.shape[0]
    token_rows = student_query.shape[1]
    split_heads = student_query.reshape(batch_count, token_rows, HEADS, HD)
    picked = jnp.take(split_heads, kept_heads, axis=2).reshape(batch_count, token_rows, KEPT * HD)
    teach_local, stud_local = (
        lax.all_to_all(teacher_query, "head", split_axis=2, concat_axis=1, tiled=True),
        lax.all_to_all(picked, "head", split_axis=2, concat_axis=1, tiled=True),
    )
    local_rows = teach_local.shape[1]
    head_count = RELH // lax.axis_size("head")
    wide_heads = batch_count * head_count
    teach_flat = batch_inside(teach_local, head_count, TREL)
    stud_flat = batch_inside(stud_local, head_count, SREL)
    position = lax.axis_index("seq")
    scales = (TREL ** (-0.5), SREL ** (-0.5))
    teach_heads = teach_flat.reshape(local_rows, wide_heads, TREL)
    stud_heads = stud_flat.reshape(local_rows, wide_heads, SREL)
    query_pos = position * local_rows + jnp.arange(local_rows, dtype=jnp.int32)
    last_query = position * local_rows + local_rows - 1
    key_pair = (
        lax.all_gather(teach_flat, "seq", axis=0, tiled=True).reshape(-1, wide_heads, TREL),
        lax.all_gather(stud_flat, "seq", axis=0, tiled=True).reshape(-1, wide_heads, SREL),
    )
    running = fold_keys(
        fresh_stats(wide_heads, local_rows),
        (teach_heads, stud_heads),
        query_pos,
        key_pair,
        last_query,
        scales,
    )
    return finish_rows(running).reshape(batch_count, head_count, local_rows)


def solution(mesh):
    placed = (P(None, ("seq", "head"), None), P(None, ("seq", "head"), None), P())
    sizes = dict(mesh.shape)

    def run(teacher, student, kept):
        batch, length = teacher.shape[0], teacher.shape[1]
        fits = (
            (sizes["seq"], sizes["head"]) == (SEQ_SIZE, HEAD_SIZE)
            and batch == 2
            and length == SEQ_SIZE * HEAD_SIZE * ROWS
        )
        step = jax.shard_map(
            packed_shards if fits else shards,
            mesh=mesh,
            in_specs=placed,
            out_specs=P(None, "head", "seq"),
            check_vma=False,
        )
        return step(teacher, student, kept)

    return run
```

```python
import functools
import math

import jax
import jax.numpy as jnp
from jax import lax
from jax.experimental import pallas as pl
from jax.experimental.pallas import tpu as pltpu
from jax.sharding import PartitionSpec as P


HEADS = 64
HD = 128
KEPT = 40
RELH = 64
TREL = 128
SREL = 80
LANES = 128
CHUNK = 32
BLOCK = 256
LIMIT = 6.0
LOG2E = math.log2(math.e)
LN2 = math.log(2.0)
SCALE_T = TREL ** (-0.5) * LOG2E
SCALE_S = SREL ** (-0.5) * LOG2E


SEQ_SIZE = 8
PACKS = ((16, 17, 18), tuple(range(16)) + tuple(range(19, 32)))
STAGES = ((0, 2), (4, 2), (2, 2), (6, 1), (7, 1))
HEAD_SIZE = 4
MESSAGE = 3 * LANES + CHUNK
UNITS = 4
ROWS = 64


def pack_kernel(numbers, kept_ref, teach_hbm, stud_hbm, *refs):
    count = len(numbers)
    outs = refs[-3 - count : -3]
    teach, heads, sems = refs[-3:]
    seq, head = lax.axis_index("seq"), lax.axis_index("head")
    lane = lax.broadcasted_iota(jnp.int32, (LANES, LANES), 1)
    small_lane = lax.broadcasted_iota(jnp.int32, (CHUNK, LANES), 1)
    copies = []
    for e, k in enumerate(numbers):
        pair = SEQ_SIZE * (head ^ (k % 4)) + (seq ^ (k // 4))
        columns = pl.ds(pl.multiple_of(pair * 2 * TREL, 2 * TREL), 2 * TREL)
        some = [pltpu.make_async_copy(teach_hbm.at[:, :, columns], teach.at[e], sems.at[e, 0])]
        for m in range(2):
            start = pl.multiple_of(kept_ref[5 * pair // 4 + m] * HD, HD)
            some.append(
                pltpu.make_async_copy(stud_hbm.at[:, :, pl.ds(start, HD)], heads.at[e, m], sems.at[e, m + 1])
            )
        for copy in some:
            copy.start()
        copies.append(some)
    for e, k in enumerate(numbers):
        for copy in copies[e]:
            copy.wait()
        i = (seq ^ (k // 4)) & 3
        out = outs[e]
        for w in range(2):
            out[w * LANES : (w + 1) * LANES, :] = teach[e, :, :, w * TREL : (w + 1) * TREL].reshape(LANES, LANES)
        first = heads[e, 0].reshape(LANES, LANES)
        last = heads[e, 1].reshape(LANES, LANES)
        out[2 * LANES : 3 * LANES, :] = jnp.where(lane >= CHUNK * i, first, last)
        extra = jnp.zeros((CHUNK, LANES), jnp.float32)
        for g in range(4):
            part = last[g * CHUNK : (g + 1) * CHUNK].astype(jnp.float32)
            if g:
                part = pltpu.roll(part, g * CHUNK, 1)
            extra = jnp.where(small_lane // CHUNK == ((i + g) & 3), part, extra)
        out[3 * LANES :, :] = extra.astype(jnp.bfloat16)


def pack(numbers, kept, teacher, student, after=()):
    anywhere = pl.BlockSpec(memory_space=pl.ANY)
    count = len(numbers)
    return pl.pallas_call(
        functools.partial(pack_kernel, numbers),
        out_shape=[jax.ShapeDtypeStruct((MESSAGE, LANES), jnp.bfloat16)] * count,
        grid_spec=pltpu.PrefetchScalarGridSpec(
            num_scalar_prefetch=1,
            grid=(1,),
            in_specs=[anywhere] * (2 + len(after)),
            out_specs=[whole_block((MESSAGE, LANES))] * count,
            scratch_shapes=[
                pltpu.VMEM((count, 2, ROWS, 2 * TREL), jnp.bfloat16),
                pltpu.VMEM((count, 2, 2, ROWS, HD), jnp.bfloat16),
                pltpu.SemaphoreType.DMA((count, 3)),
            ],
        ),
    )(kept, teacher, student, *after)


def whole_block(shape):
    return pl.BlockSpec(shape, lambda *_: (0,) * len(shape), pipeline_mode=pl.Buffered(1))


def nt_dot(a, b):
    return lax.dot_general(a, b, (((1,), (1,)), ((), ())), preferred_element_type=jnp.float32)


def shift_of(rows, width, factor):
    norm = jnp.sqrt(nt_dot(jnp.ones((8, LANES), jnp.bfloat16), rows * rows))
    return norm * (norm + LIMIT * math.sqrt(width)) * (0.5 * factor)


def split_terms(row, scale):
    scaled = row * scale
    high = scaled.astype(jnp.bfloat16)
    return high, (scaled - high.astype(jnp.float32)).astype(jnp.bfloat16)


def prepared_shapes(blocks):
    count = blocks * BLOCK
    bf16 = jnp.bfloat16
    return [
        ((UNITS, count, LANES), bf16),
        ((UNITS, count, LANES), bf16),
        ((UNITS, count, 2 * LANES), bf16),
        ((UNITS, count, 2 * LANES), bf16),
        ((UNITS, 2, blocks, 8, BLOCK), jnp.float32),
    ]


def prepare(messages, made):
    key_t, key_s, query_t, query_s, shifts = made
    lane = lax.broadcasted_iota(jnp.int32, (ROWS, LANES), 1)
    rel = (lane - CHUNK * (lax.axis_index("seq") & 3)) & (LANES - 1)
    in_first = rel < SREL
    in_tail = rel < CHUNK
    zero = jnp.zeros((ROWS, LANES), jnp.float32)
    for k, message in enumerate(messages):
        start = (k // 4) * BLOCK + (lax.axis_index("head") ^ (k % 4)) * ROWS
        at = pl.ds(pl.multiple_of(start, ROWS), ROWS)
        tail = message[3 * LANES :, :].astype(jnp.float32)
        for b in range(2):
            main = message[2 * LANES + b * ROWS : 2 * LANES + (b + 1) * ROWS, :].astype(jnp.float32)
            parts = [
                pltpu.roll(tail, LANES - g * CHUNK, 1) if g else tail for g in (2 * b, 2 * b + 1)
            ]
            own = jnp.concatenate(parts, axis=0)
            both = (jnp.where(in_first, main, zero), jnp.where(in_tail, own, jnp.where(in_first, zero, main)))
            for w in range(2):
                u = 2 * b + w
                key = message[w * LANES + b * ROWS : w * LANES + (b + 1) * ROWS, :]
                key_t[u, at, :] = key
                query_t[u, at, 0:LANES], query_t[u, at, LANES:] = split_terms(key.astype(jnp.float32), SCALE_T)
                key_s[u, at, :] = both[w].astype(jnp.bfloat16)
                query_s[u, at, 0:LANES], query_s[u, at, LANES:] = split_terms(both[w], SCALE_S)

    def shift(u, carry):
        for block in range(len(messages) // 4):
            rows = slice(block * BLOCK, (block + 1) * BLOCK)
            shifts[u, 0, block] = shift_of(key_t[u, rows, :], TREL, SCALE_T)
            shifts[u, 1, block] = shift_of(key_s[u, rows, :], SREL, SCALE_S)
        return carry

    for u in range(UNITS):
        shift(u, 0)


def tile_sums(u, keys, key_block, queries, query_block, allowed=None):
    rows = pl.ds(pl.multiple_of(key_block * BLOCK, BLOCK), BLOCK)
    cols = pl.ds(pl.multiple_of(query_block * BLOCK, BLOCK), BLOCK)
    tile = (BLOCK // 8, 8, BLOCK)
    key_t, key_s = keys[0][u, rows, :], keys[1][u, rows, :]
    x_t = nt_dot(jnp.concatenate([key_t, key_t], axis=1), queries[2][u, cols, :])
    x_s = nt_dot(jnp.concatenate([key_s, key_s], axis=1), queries[3][u, cols, :])
    x_t = x_t.reshape(tile) - queries[4][u, 0, query_block][None]
    x_s = x_s.reshape(tile) - queries[4][u, 1, query_block][None]
    w_t = jnp.exp2(x_t)
    w_s = jnp.exp2(x_s)
    if allowed is not None:
        w_t = jnp.where(allowed, w_t, 0.0)
        w_s = jnp.where(allowed, w_s, 0.0)
    return jnp.sum(w_t, axis=0), jnp.sum(w_t * (x_t - x_s), axis=0), jnp.sum(w_s, axis=0)


def causal_tile():
    tile = (BLOCK // 8, 8, BLOCK)
    key_in = lax.broadcasted_iota(jnp.int32, tile, 0) * 8 + lax.broadcasted_iota(jnp.int32, tile, 1)
    return key_in <= lax.broadcasted_iota(jnp.int32, tile, 2)


def over_units(tiles, body):
    some = max(1, min(UNITS, 8 // tiles))

    def step(i, carry):
        for j in range(some):
            body(i * some + j)
        return carry

    if some == UNITS:
        step(0, 0)
    else:
        lax.fori_loop(0, UNITS // some, step, 0)


def add_to(sums, slot, u, more):
    for i in range(3):
        sums[slot, u, i] += more[i]


def pairs_inside(seq, base, blocks, made, sums):
    allowed = causal_tile()

    def unit(u):
        for m in range(blocks):
            for n in range(m + 1, blocks):
                ahead = (seq ^ (base + m)) < (seq ^ (base + n))
                key_block = jnp.where(ahead, m, n)
                query_block = jnp.where(ahead, n, m)
                add_to(sums, base + query_block, u, tile_sums(u, made, key_block, made, query_block))
        for m in range(blocks):
            add_to(sums, base + m, u, tile_sums(u, made, m, made, m, allowed))

    over_units(blocks * (blocks + 1) // 2, unit)


def pairs_between(seq, old_base, old_blocks, old, new_base, new_blocks, new, sums):
    ahead = (seq ^ old_base) < (seq ^ new_base)

    def old_keys(u):
        for n in range(new_blocks):
            parts = [tile_sums(u, old, m, new, n) for m in range(old_blocks)]
            add_to(sums, new_base + n, u, [sum(part[i] for part in parts) for i in range(3)])

    def new_keys(u):
        for m in range(old_blocks):
            parts = [tile_sums(u, new, n, old, m) for n in range(new_blocks)]
            add_to(sums, old_base + m, u, [sum(part[i] for part in parts) for i in range(3)])

    @pl.when(ahead)
    def _():
        over_units(old_blocks * new_blocks, old_keys)

    @pl.when(jnp.logical_not(ahead))
    def _():
        over_units(old_blocks * new_blocks, new_keys)


def stage_kernel(base, blocks, older, last, *refs):
    messages, refs = refs[: 4 * blocks], refs[4 * blocks :]
    sets = []
    for start, size in older:
        sets.append((start, size, refs[:5]))
        refs = refs[5:]
    before = None
    if older:
        before, refs = refs[0], refs[1:]
    if last:
        out_ref, made, sums = refs[0], refs[1:6], refs[6]
    else:
        made, sums = refs[:5], refs[5]
    seq = lax.axis_index("seq")
    sums[...] = jnp.zeros(sums.shape, jnp.float32) if before is None else before[...]
    prepare(messages, made)
    for start, size, old in sets:
        pairs_between(seq, start, size, old, base, blocks, made, sums)
    pairs_inside(seq, base, blocks, made, sums)
    if last:
        for m in range(SEQ_SIZE):
            total = jnp.sum(sums[m], axis=2)
            total_t, total_c, total_s = total[:, 0], total[:, 1], total[:, 2]
            out_ref[seq ^ m] = (total_c / total_t - jnp.log2(total_t) + jnp.log2(total_s)) * LN2


def stage(base, blocks, older, messages, old_sets, before, last=False):
    made_shapes = prepared_shapes(blocks)
    sums_shape = (SEQ_SIZE, UNITS, 3, 8, BLOCK)
    out_shape = (SEQ_SIZE, UNITS, BLOCK)
    if last:
        outs, scratch = [(out_shape, jnp.float32)], made_shapes + [(sums_shape, jnp.float32)]
    else:
        outs, scratch = made_shapes + [(sums_shape, jnp.float32)], []
    inputs = list(messages) + [array for old in old_sets for array in old] + ([before] if older else [])
    return pl.pallas_call(
        functools.partial(stage_kernel, base, blocks, older, last),
        out_shape=[jax.ShapeDtypeStruct(shape, dtype) for shape, dtype in outs],
        grid_spec=pl.GridSpec(
            grid=(1,),
            in_specs=[whole_block(array.shape) for array in inputs],
            out_specs=[whole_block(shape) for shape, _ in outs],
            scratch_shapes=[pltpu.VMEM(shape, dtype) for shape, dtype in scratch],
        ),
        compiler_params=pltpu.CompilerParams(vmem_limit_bytes=24 * 1024 * 1024),
    )(*inputs)


def packed_shards(teacher, student, kept):
    batch = teacher.shape[0]

    def exchange(message, k):
        pairs = [(i, i ^ k) for i in range(SEQ_SIZE * HEAD_SIZE)]
        return lax.ppermute(message, ("seq", "head"), pairs)

    packed, got, after = {}, {}, ()
    for numbers in PACKS:
        packed.update(zip(numbers, pack(numbers, kept, teacher, student, after)))
        after = (packed[numbers[-1]],)
    got[0] = packed[0]
    for k in range(1, 32):
        got[k] = exchange(packed[k], k)
    messages = [got[k] for k in range(32)]
    older, sums = [], None
    for base, blocks in STAGES:
        *made, sums = stage(
            base,
            blocks,
            tuple(entry[:2] for entry in older),
            messages[4 * base : 4 * (base + blocks)],
            [entry[2] for entry in older],
            sums,
            last=(base, blocks) == STAGES[-1],
        )
        older.append((base, blocks, made))
    mine = sums
    done = lax.all_to_all(mine, "seq", 0, 0, tiled=True)
    pair = RELH // HEAD_SIZE // SEQ_SIZE
    done = done.reshape(SEQ_SIZE, batch, pair, BLOCK)
    return jnp.transpose(done, (1, 0, 2, 3)).reshape(batch, RELH // HEAD_SIZE, BLOCK)


NEG_FILL = -1e30


def fresh_stats(head_count, query_count):
    lowest = jnp.full((head_count, query_count), NEG_FILL, jnp.float32)
    zeros_block = jnp.zeros((head_count, query_count), jnp.float32)
    return (lowest, zeros_block, zeros_block, lowest, zeros_block)


def relation_update(running, query_pair, key_pair, query_pos, key_pos, scales):
    top_t, total_t, cross_sum, top_s, total_s = running
    teach_scores = (
        jnp.einsum("qhd,khd->hqk", query_pair[0], key_pair[0], preferred_element_type=jnp.float32)
        * scales[0]
    )
    stud_scores = (
        jnp.einsum("qhd,khd->hqk", query_pair[1], key_pair[1], preferred_element_type=jnp.float32)
        * scales[1]
    )
    allowed = key_pos[None, :] <= query_pos[:, None]
    teach_scores = jnp.where(allowed[None], teach_scores, NEG_FILL)
    stud_scores = jnp.where(allowed[None], stud_scores, NEG_FILL)
    new_top_t = jnp.maximum(top_t, jnp.max(teach_scores, axis=2))
    new_top_s = jnp.maximum(top_s, jnp.max(stud_scores, axis=2))
    weights_t = jnp.exp(teach_scores - new_top_t[:, :, None])
    weights_s = jnp.exp(stud_scores - new_top_s[:, :, None])
    decay_t = jnp.exp(top_t - new_top_t)
    decay_s = jnp.exp(top_s - new_top_s)
    total_t = total_t * decay_t + jnp.sum(weights_t, axis=2)
    cross_sum = cross_sum * decay_t + jnp.sum(weights_t * (teach_scores - stud_scores), axis=2)
    total_s = total_s * decay_s + jnp.sum(weights_s, axis=2)
    return (new_top_t, total_t, cross_sum, new_top_s, total_s)


def finish_rows(running):
    top_t, total_t, cross_sum, top_s, total_s = running
    return cross_sum / total_t - top_t - jnp.log(total_t) + top_s + jnp.log(total_s)


def fold_keys(running, query_pair, query_pos, key_pair, last_query, scales):
    key_length = key_pair[0].shape[0]
    key_block = 512
    steps_total = key_length // key_block

    def one_block(block_number, current):
        row_start = block_number * key_block
        block_t = lax.dynamic_slice_in_dim(key_pair[0], row_start, key_block, 0)
        block_s = lax.dynamic_slice_in_dim(key_pair[1], row_start, key_block, 0)
        key_pos = row_start + jnp.arange(key_block, dtype=jnp.int32)
        return relation_update(current, query_pair, (block_t, block_s), query_pos, key_pos, scales)

    needed = jnp.clip(last_query // key_block + 1, 0, steps_total)
    return lax.fori_loop(0, needed, one_block, running)


def batch_inside(local, head_count, width):
    seq_count_b, rows, _ = local.shape
    folded = local.reshape(seq_count_b, rows, head_count, width)
    return jnp.transpose(folded, (1, 0, 2, 3)).reshape(rows, seq_count_b * head_count * width)


def shards(teacher_query, student_query, kept_heads):
    batch_count = student_query.shape[0]
    token_rows = student_query.shape[1]
    split_heads = student_query.reshape(batch_count, token_rows, HEADS, HD)
    picked = jnp.take(split_heads, kept_heads, axis=2).reshape(batch_count, token_rows, KEPT * HD)
    teach_local, stud_local = (
        lax.all_to_all(teacher_query, "head", split_axis=2, concat_axis=1, tiled=True),
        lax.all_to_all(picked, "head", split_axis=2, concat_axis=1, tiled=True),
    )
    local_rows = teach_local.shape[1]
    head_count = RELH // lax.axis_size("head")
    wide_heads = batch_count * head_count
    teach_flat = batch_inside(teach_local, head_count, TREL)
    stud_flat = batch_inside(stud_local, head_count, SREL)
    position = lax.axis_index("seq")
    scales = (TREL ** (-0.5), SREL ** (-0.5))
    teach_heads = teach_flat.reshape(local_rows, wide_heads, TREL)
    stud_heads = stud_flat.reshape(local_rows, wide_heads, SREL)
    query_pos = position * local_rows + jnp.arange(local_rows, dtype=jnp.int32)
    last_query = position * local_rows + local_rows - 1
    key_pair = (
        lax.all_gather(teach_flat, "seq", axis=0, tiled=True).reshape(-1, wide_heads, TREL),
        lax.all_gather(stud_flat, "seq", axis=0, tiled=True).reshape(-1, wide_heads, SREL),
    )
    running = fold_keys(
        fresh_stats(wide_heads, local_rows),
        (teach_heads, stud_heads),
        query_pos,
        key_pair,
        last_query,
        scales,
    )
    return finish_rows(running).reshape(batch_count, head_count, local_rows)


def solution(mesh):
    placed = (P(None, ("seq", "head"), None), P(None, ("seq", "head"), None), P())
    sizes = dict(mesh.shape)

    def run(teacher, student, kept):
        batch, length = teacher.shape[0], teacher.shape[1]
        fits = (
            (sizes["seq"], sizes["head"]) == (SEQ_SIZE, HEAD_SIZE)
            and batch == 2
            and length == SEQ_SIZE * HEAD_SIZE * ROWS
        )
        step = jax.shard_map(
            packed_shards if fits else shards,
            mesh=mesh,
            in_specs=placed,
            out_specs=P(None, "head", "seq"),
            check_vma=False,
        )
        return step(teacher, student, kept)

    return run
```
